256 devices in a mesh: hel: 16 (over x_hi, z), rad: 16 (over x_lo, y, core).
Axes of the slice: x: 4 (x_hi: 2, x_lo: 2; x = x_hi * 2 + x_lo), y: 4, z: 8, core: 2. Of those that a mesh axis runs over, the one named last changes fastest.
Arguments:
- psi_start: float32 [16, 256, 16, 768], P('hel', 'rad'), may hold values from -6 to 6
- potential: float32 [256, 16, 1536], P('rad'), may hold values from -0.5 to 0.5
- basis: bfloat16 [768, 1536], replicated, may hold values from -0.21875 to 0.21875
- kinetic: bfloat16 [256, 256], replicated, may hold values from -0.375 to 0.375
- radial_factor: float32 [256], P('rad'), may hold values from 0.002 to 0.02
- damping: float32 [256], P('rad'), may hold values from 0.7 to 1
- coupling: bfloat16 [16, 768], P('hel'), may hold values from -2 to 2
- helicity: int32 [16], P('hel'), may hold values from 0 to 7
- chan_rad: int32 [1024], replicated, may hold values from 0 to 255
- chan_vib: int32 [1024], replicated, may hold values from 0 to 15
- projector: bfloat16 [1024, 768], replicated, may hold values from -0.21875 to 0.21875
Outputs:
- psi_final: float32 [16, 256, 16, 768], P('hel', 'rad')
- amplitude: float32 [16, 1024], P('hel', 'rad')
The draws below stay inside these ranges and needn't reach their ends.
All inputs are finite; a program needn't handle non-finite values.
Results may differ from the reference program's by a relative error of at most 0.0046.
Values may be sent and summed in bfloat16 or wider, within the bound.
A program may use at most 64 MiB of HBM per device.

```python
import math
import jax
import jax.numpy as jnp
from jax import lax

NV = 16
J = 768
Q = 1536
CH = 1024
ITERS = 3
HEL = 16
NR = 256


def touch_ends(result, key, smallest, largest):
    extent = result.shape
    place = [jax.random.randint(jax.random.fold_in(key, axis), (), 0, extent[axis]) for axis in range(len(extent))]
    result = result.at[tuple(place)].set(smallest)
    longest = extent.index(max(extent))
    place[longest] = (place[longest] + 1) % extent[longest]
    return result.at[tuple(place)].set(largest)


def shard_levels(own_key, shape, shards, low, largest):
    def one(dim, parts):
        draws = jax.random.uniform(jax.random.fold_in(jax.random.fold_in(own_key, 6), dim), (parts,), jnp.float32, low / len(shards), largest / len(shards))
        return jnp.repeat(jnp.exp(draws), shape[dim] // parts).reshape((-1,) + (1,) * (len(shape) - dim - 1))

    level = one(*shards[0])
    for cut in shards[1:]:
        level = level * one(*cut)
    return level


def scatter_about(rng, extent, scale, reach, split=(), held_as=jnp.bfloat16):
    drawn = jax.random.normal(rng, extent, jnp.float32) * scale
    if len(split) > 0:
        drawn = shard_levels(rng, extent, split, -0.22, 0.18) * drawn
    return jnp.clip(drawn, min=-reach, max=reach).astype(held_as)


def setup_inputs(seed: int = 0) -> dict:
    arg_keys = jax.random.split(jax.random.key(seed), 12)
    psi_start = scatter_about(arg_keys[0], (HEL, NR, NV, J), 1.0, 6.0, ((0, 16), (1, 16)), jnp.float32)
    potential = jnp.clip(jax.random.uniform(arg_keys[1], (NR, NV, Q), jnp.float32, -0.5, 0.5) * shard_levels(arg_keys[1], (NR, NV, Q), ((0, 16),), -0.4, 0.0), -0.5, 0.5)
    basis = scatter_about(arg_keys[2], (J, Q), J ** -0.5, 0.21875)
    kinetic = scatter_about(arg_keys[3], (NR, NR), NR ** -0.5, 0.375)
    radial_factor = jnp.clip(jnp.exp(math.log(0.02) - 2.30258502 * jax.random.uniform(arg_keys[4], (NR,), jnp.float32) ** shard_levels(arg_keys[4], (NR,), ((0, 16),), -0.2, 0.2)), 0.002, 0.02)
    damping = jnp.clip(0.7 + 0.3 * jax.random.uniform(arg_keys[5], (NR,), jnp.float32) ** shard_levels(arg_keys[5], (NR,), ((0, 16),), -0.2, 0.2), 0.7, 1.0)
    coupling = scatter_about(arg_keys[6], (HEL, J), 0.3, 2.0, ((0, 16),))
    helicity = touch_ends(jax.random.randint(arg_keys[7], (HEL,), 0, 8), jax.random.fold_in(arg_keys[7], 1), 0, 7).astype(jnp.int32)
    chan_rad = touch_ends(jax.random.randint(arg_keys[8], (CH,), 0, NR), jax.random.fold_in(arg_keys[8], 1), 0, NR - 1).astype(jnp.int32)
    chan_vib = touch_ends(jax.random.randint(arg_keys[9], (CH,), 0, NV), jax.random.fold_in(arg_keys[9], 1), 0, NV - 1).astype(jnp.int32)
    projector = scatter_about(arg_keys[10], (CH, J), J ** -0.5, 0.21875)
    return {"psi_start": psi_start, "potential": potential, "basis": basis, "kinetic": kinetic, "radial_factor": radial_factor, "damping": damping, "coupling": coupling, "helicity": helicity, "chan_rad": chan_rad, "chan_vib": chan_vib, "projector": projector}


def apply_ham(psi, potential, basis, kinetic, radial_factor, coupling_eff, coupling_prev, kvalue):
    packed = psi.astype(jnp.bfloat16)
    packed_f = packed.astype(jnp.float32)
    kin = jnp.einsum('rs,ksvj->krvj', kinetic.astype(jnp.float32), packed_f)

    def angular(block):
        grid = jnp.dot(block.reshape(NR * NV, J), basis, preferred_element_type=jnp.float32)
        scaled = (grid * potential.reshape(NR * NV, Q)).astype(jnp.bfloat16)
        back = lax.dot_general(scaled, basis, (((1,), (1,)), ((), ())), preferred_element_type=jnp.float32)
        return back.reshape(NR, NV, J)

    ang = lax.map(angular, packed)
    zero = jnp.zeros((1, NR, NV, J), jnp.float32)
    upper = jnp.concatenate([packed_f[1:], zero], axis=0)
    lower = jnp.concatenate([zero, packed_f[:-1]], axis=0)
    cor = coupling_eff[:, None, None, :] * upper + coupling_prev[:, None, None, :] * lower
    cen = -2.0 * (kvalue * kvalue)[:, None, None, None] * radial_factor[None, :, None, None] * psi
    return kin + ang + cen + cor


def reference(psi_start, potential, basis, kinetic, radial_factor, damping, coupling, helicity, chan_rad, chan_vib, projector):
    keep = (jnp.arange(HEL) < HEL - 1).astype(jnp.float32)
    coupling_eff = coupling.astype(jnp.float32) * keep[:, None]
    coupling_prev = jnp.concatenate([jnp.zeros((1, J), jnp.float32), coupling_eff[:-1]], axis=0)
    kvalue = helicity.astype(jnp.float32)
    damp = damping[None, :, None, None]

    def ham(p):
        return apply_ham(p, potential, basis, kinetic, radial_factor, coupling_eff, coupling_prev, kvalue)

    previous = psi_start
    current = damp * ham(psi_start)
    for step in range(ITERS - 1):
        following = damp * (2.0 * ham(current) - damp * previous)
        previous, current = current, following
    final_b = current.astype(jnp.bfloat16).astype(jnp.float32)
    rows = final_b[:, chan_rad, chan_vib, :]
    amplitude = jnp.sum(rows * projector.astype(jnp.float32)[None], axis=-1)
    return current, amplitude
```

```python
import jax
import jax.numpy as jnp
from jax import lax
from jax.sharding import PartitionSpec as P

ITERS = 3


def from_behind(block, axis, distance):
    devices = range(lax.axis_size(axis))
    route = [(i - distance, i) for i in devices if i - distance in devices]
    return lax.ppermute(block, axis, route)


def per_device(
    psi_start,
    potential,
    basis,
    kinetic,
    radial_factor,
    damping,
    coupling,
    helicity,
    chan_rad,
    chan_vib,
    projector,
):
    _, rdev, nvib, nang = psi_start.shape
    nquad = basis.shape[1]
    rad_index = lax.axis_index("rad")
    hel_index = lax.axis_index("hel")
    last = lax.axis_size("hel") - 1
    coupling_eff = jnp.where(hel_index < last, coupling, jnp.zeros_like(coupling))
    coupling_prev = from_behind(coupling_eff, "hel", 1).astype(jnp.float32)
    coupling_eff = coupling_eff.astype(jnp.float32)
    kvalue = helicity.astype(jnp.float32)[0]
    scales = lax.all_gather(jnp.stack([radial_factor, damping]), "rad", axis=1, tiled=True)
    cen_factor = (-2.0 * kvalue * kvalue * scales[0])[:, None]
    damp = scales[1][:, None]
    psi = lax.all_to_all(
        psi_start[0].astype(jnp.bfloat16), "rad", split_axis=1, concat_axis=0, tiled=True
    ).reshape(-1, nang)
    pot = lax.all_to_all(
        potential.astype(jnp.bfloat16), "rad", split_axis=1, concat_axis=0, tiled=True
    ).reshape(-1, nquad)

    def ham(psi):
        packed = psi.astype(jnp.bfloat16)
        lower = from_behind(packed, "hel", 1).astype(jnp.float32)
        upper = from_behind(packed, "hel", -1).astype(jnp.float32)
        kin = jnp.dot(kinetic, packed, preferred_element_type=jnp.float32)
        grid = jnp.dot(packed, basis, preferred_element_type=jnp.float32)
        scaled = (grid * pot).astype(jnp.bfloat16)
        ang = lax.dot_general(
            scaled, basis, (((1,), (1,)), ((), ())), preferred_element_type=jnp.float32
        )
        cor = coupling_eff * upper + coupling_prev * lower
        return kin + ang + cen_factor * psi + cor

    previous = psi.astype(jnp.float32)
    current = damp * ham(previous)
    for step in range(ITERS - 1):
        following = damp * (2.0 * ham(current) - damp * previous)
        previous, current = (current, following)
    final_b = current.astype(jnp.bfloat16)
    back = lax.all_to_all(
        final_b.reshape(-1, 1, nang), "rad", split_axis=0, concat_axis=1, tiled=True
    )
    psi_final = back.astype(jnp.float32)[None]
    hits = lax.dot_general(
        projector, final_b, (((1,), (1,)), ((), ())), preferred_element_type=jnp.float32
    )
    slot = jnp.where(chan_vib == rad_index, chan_rad, -1)
    chosen = slot[:, None] == jnp.arange(final_b.shape[0], dtype=jnp.int32)[None, :]
    partial_amp = jnp.sum(jnp.where(chosen, hits, 0.0), axis=1)
    tiles = partial_amp.reshape(lax.axis_size("rad"), -1)
    arrived = lax.all_to_all(tiles, "rad", split_axis=0, concat_axis=0, tiled=True)
    amplitude = arrived.sum(axis=0)[None]
    return (psi_final, amplitude)


def solution(mesh):
    placed = (
        P("hel", "rad", None, None),
        P("rad", None, None),
        P(),
        P(),
        P("rad"),
        P("rad"),
        P("hel", None),
        P("hel"),
        P(),
        P(),
        P(),
    )
    return jax.shard_map(
        per_device,
        mesh=mesh,
        in_specs=placed,
        out_specs=(P("hel", "rad", None, None), P("hel", "rad")),
        check_vma=False,
    )
```

```python
import jax
import jax.numpy as jnp
from jax import lax
from jax.experimental import pallas as pl
from jax.experimental.pallas import tpu as pltpu
from jax.sharding import PartitionSpec as P

ITERS = 3
MESH = pl.DeviceIdType.MESH
F32 = jnp.float32
BF16 = jnp.bfloat16
NCH = 16
ZS = 8
LANES = 128


def kernel(
    psi_hbm,
    pot_hbm,
    basis_hbm,
    kin_hbm,
    proj_hbm,
    rf_s,
    damp_s,
    hel_s,
    coup_ref,
    crad_ref,
    cvib_ref,
    fin_ref,
    amp_ref,
    psi_v,
    pot_v,
    basis,
    kin,
    proj,
    stage,
    pstage,
    tile,
    tiles,
    ce,
    cp,
    pb,
    lo,
    up,
    fw,
    pot,
    scaled,
    tot,
    dmp,
    cen,
    asend,
    arecv,
    load_sem,
    psi_l,
    pot_l,
    psi_s,
    psi_r,
    til_s,
    til_r,
    pot_s,
    pot_r,
    sib_s,
    sib_r,
    lo_s,
    lo_r,
    up_s,
    up_r,
    cp_s,
    cp_r,
    fin_s,
    fin_r,
    amp_s,
    amp_r,
):
    hel, rad = lax.axis_index("hel"), lax.axis_index("rad")
    x_hi, z = hel // ZS, hel % ZS
    x_lo, y, core = rad // 8, (rad // 2) % 4, rad % 2
    v_me = x_hi * 8 + x_lo * 4 + y
    k_me = core * ZS + z
    above = (x_hi * ZS + (z + 1) % ZS, x_lo * 8 + y * 2 + (core + (z + 1) // ZS) % 2)
    below = (
        x_hi * ZS + (z + ZS - 1) % ZS,
        x_lo * 8 + y * 2 + (core + 1 - (z + ZS - 1) // ZS) % 2,
    )
    sibling = (hel, x_lo * 8 + y * 2 + 1 - core)
    rows, nang = pb.shape[1:]
    nquad = pot.shape[1]
    part = rows // NCH

    def load_lanes(b, carry):
        cols = pl.ds(pl.multiple_of(b * LANES, LANES), LANES)
        pltpu.make_async_copy(psi_hbm.at[:, cols], psi_v.at[b], psi_l.at[b]).start()
        return carry

    def load_pot_lanes(b, carry):
        cols = pl.ds(pl.multiple_of(b * LANES, LANES), LANES)
        pltpu.make_async_copy(pot_hbm.at[:, cols], pot_v.at[b], pot_l.at[b]).start()
        return carry

    lax.fori_loop(0, nang // LANES, load_lanes, 0)
    lax.fori_loop(0, nquad // LANES, load_pot_lanes, 0)
    loads = [
        pltpu.make_async_copy(src, dst, load_sem.at[i])
        for i, (src, dst) in enumerate([(kin_hbm, kin), (basis_hbm, basis), (proj_hbm, proj)])
    ]
    for load in loads:
        load.start()

    barrier = pltpu.get_barrier_semaphore()
    here = x_hi * NCH + rad

    def greet(i, carry):
        other = (here + 1 + i) % (2 * NCH)
        pl.semaphore_signal(
            barrier,
            inc=1,
            device_id=((other // NCH) * ZS + z, other % NCH),
            device_id_type=MESH,
        )
        return carry

    lax.fori_loop(0, 2 * NCH - 1, greet, 0)
    for neighbour in (above, below):
        pl.semaphore_signal(barrier, inc=1, device_id=neighbour, device_id_type=MESH)

    def chunk(i):
        return pl.ds(pl.multiple_of(i * part, part), part)

    def remote(src, dst, send, recv, device):
        return pltpu.make_async_remote_copy(
            src_ref=src,
            dst_ref=dst,
            send_sem=send,
            recv_sem=recv,
            device_id=device,
            device_id_type=MESH,
        )

    def is_here(device):
        return (device[0] == hel) & (device[1] == rad)

    def push(src, dst, send, recv, device):
        mine = is_here(device)

        @pl.when(mine)
        def _():
            pltpu.make_async_copy(src, dst, recv).start()

        @pl.when(jnp.logical_not(mine))
        def _():
            remote(src, dst, send, recv, device).start()

    def pushed(src, dst, send, recv, device):
        @pl.when(jnp.logical_not(is_here(device)))
        def _():
            remote(src, dst, send, recv, device).wait_send()

    sub = lax.broadcasted_iota(jnp.int32, (8, LANES), 0)
    lane = lax.broadcasted_iota(jnp.int32, (8, LANES), 1)
    kvalue = hel_s[0].astype(F32)
    small = jnp.zeros((8, LANES), F32)
    for i in range(part):
        small = jnp.where((sub == 0) & (lane == i), damp_s[i], small)
        small = jnp.where(
            (sub == 0) & (lane == part + i), -2.0 * (kvalue * kvalue) * rf_s[i], small
        )
    tile[...] = small
    wide = coup_ref[...].astype(F32)
    for b in range(nang // LANES):
        tile[2 + b : 3 + b, :] = wide[:, b * LANES : (b + 1) * LANES]

    for b in range(nang // LANES):
        cols = slice(b * LANES, (b + 1) * LANES)
        pltpu.make_async_copy(psi_hbm.at[:, cols], psi_v.at[b], psi_l.at[b]).wait()
        for v in range(NCH):
            stage[v, :, cols] = psi_v[b, pl.ds(v, part, stride=NCH), :].astype(BF16)
    pl.semaphore_wait(barrier, 2 * NCH + 1)

    def holder(s):
        v = (rad + s) % NCH
        return v, ((v // 8) * ZS + z, v % 8 * 2 + x_hi)

    def send_psi(s, carry):
        v, device = holder(s)
        push(stage.at[v], pb.at[0, chunk(rad), :], psi_s.at[s], psi_r.at[rad], device)
        return carry

    def send_tile(s, carry):
        v, device = holder(s)
        push(tile, tiles.at[rad], til_s.at[s], til_r.at[rad], device)
        return carry

    lax.fori_loop(0, NCH, send_psi, 0)
    lax.fori_loop(0, NCH, send_tile, 0)

    for b in range(nquad // LANES):
        cols = slice(b * LANES, (b + 1) * LANES)
        pltpu.make_async_copy(pot_hbm.at[:, cols], pot_v.at[b], pot_l.at[b]).wait()
        for i in range(NCH // 2):
            pstage[i, :, cols] = pot_v[b, pl.ds(x_hi * 8 + i, part, stride=NCH), :].astype(BF16)

    def pot_holder(s):
        i = (rad // 2 + s) % 8
        return i, (hel, 2 * i + core)

    def send_pot(s, carry):
        i, device = pot_holder(s)
        push(pstage.at[i], pot.at[chunk(rad), :], pot_s.at[s], pot_r.at[rad // 2], device)
        return carry

    lax.fori_loop(0, NCH // 2, send_pot, 0)

    def send_on(n, i):
        remote(
            pb.at[n, chunk(i), :], lo.at[n, chunk(i), :], lo_s.at[n, i], lo_r.at[n, i], above
        ).start()
        remote(
            pb.at[n, chunk(i), :], up.at[n, chunk(i), :], up_s.at[n, i], up_r.at[n, i], below
        ).start()

    def order(s):
        return (v_me + NCH - s) % NCH

    def take_psi(s, carry):
        i = order(s)
        pltpu.make_async_copy(stage.at[0], pb.at[0, chunk(i), :], psi_r.at[i]).wait()
        send_on(0, i)
        return carry

    lax.fori_loop(0, NCH, take_psi, 0)

    diag = lax.broadcasted_iota(jnp.int32, (part, LANES), 0)
    diag_lane = lax.broadcasted_iota(jnp.int32, (part, LANES), 1)

    def take_tile(i, carry):
        pltpu.make_async_copy(tile, tiles.at[i], til_r.at[i]).wait()
        row = jnp.broadcast_to(tiles[i, 0:1, :], (part, LANES))
        d = jnp.sum(jnp.where(diag_lane == diag, row, 0.0), axis=1, keepdims=True)
        c = jnp.sum(jnp.where(diag_lane == diag + part, row, 0.0), axis=1, keepdims=True)
        dmp[chunk(i), :] = jnp.broadcast_to(d, (part, LANES))
        cen[chunk(i), :] = jnp.broadcast_to(c, (part, LANES))
        return carry

    lax.fori_loop(0, NCH, take_tile, 0)
    ce[...] = jnp.where(k_me < 2 * ZS - 1, tiles[0], 0.0)
    remote(ce, cp, cp_s, cp_r, above).start()

    fw[0] = jnp.zeros((rows, nang), F32)
    fw[1] = pb[0].astype(F32)

    def take_pot(s, carry):
        j = (v_me % 8 + 8 - s) % 8
        i = 2 * j + core
        pltpu.make_async_copy(pstage.at[0], pot.at[chunk(i), :], pot_r.at[j]).wait()
        remote(
            pot.at[chunk(i), :], pot.at[chunk(i), :], sib_s.at[j], sib_r.at[j], sibling
        ).start()
        return carry

    lax.fori_loop(0, NCH // 2, take_pot, 0)
    for load in loads:
        load.wait()

    def take_sib(j, carry):
        i = 2 * j + 1 - core
        pltpu.make_async_copy(pstage.at[0], pot.at[chunk(i), :], sib_r.at[j]).wait()
        return carry

    lax.fori_loop(0, NCH // 2, take_sib, 0)
    remote(ce, cp, cp_s, cp_r, above).wait()

    wide_q = 256

    def step(n, carry):
        for q in range(nquad // wide_q):
            cols = slice(q * wide_q, (q + 1) * wide_q)
            grid = jnp.dot(pb[n], basis[:, cols], preferred_element_type=F32)
            scaled[:, cols] = (grid * pot[:, cols].astype(F32)).astype(BF16)
        for q in range(nang // wide_q):
            cols = slice(q * wide_q, (q + 1) * wide_q)
            tot[:, cols] = jnp.dot(
                kin[...], pb[n, :, cols], preferred_element_type=F32
            ) + lax.dot_general(
                scaled[...],
                basis[cols, :],
                (((1,), (1,)), ((), ())),
                preferred_element_type=F32,
            )
        gain = jnp.where(n == 0, 1.0, 2.0).astype(F32)

        def finish(s, carry):
            i = order(s)
            pltpu.make_async_copy(stage.at[0], lo.at[n, chunk(i), :], lo_r.at[n, i]).wait()
            pltpu.make_async_copy(stage.at[0], up.at[n, chunk(i), :], up_r.at[n, i]).wait()
            d = dmp[chunk(i), :]
            c = cen[chunk(i), :]
            for b in range(nang // LANES):
                cols = slice(b * LANES, (b + 1) * LANES)
                h = (
                    tot[chunk(i), cols]
                    + c * fw[n + 1, chunk(i), cols]
                    + ce[2 + b : 3 + b, :] * up[n, chunk(i), cols].astype(F32)
                    + cp[2 + b : 3 + b, :] * lo[n, chunk(i), cols].astype(F32)
                )
                new = d * (gain * h - d * fw[n, chunk(i), cols])
                fw[n + 2, chunk(i), cols] = new
                pb[n + 1, chunk(i), cols] = new.astype(BF16)

            @pl.when(n < ITERS - 1)
            def _():
                send_on(n + 1, i)

            @pl.when(n == ITERS - 1)
            def _():
                push(
                    fw.at[ITERS + 1, chunk(i), :],
                    fin_ref.at[v_me],
                    fin_s.at[i],
                    fin_r.at[v_me],
                    (k_me, i),
                )

            return carry

        lax.fori_loop(0, NCH, finish, 0)
        return carry

    lax.fori_loop(0, ITERS, step, 0)

    radial = lax.broadcasted_iota(jnp.int32, (rows, LANES), 0)
    for b in range(crad_ref.shape[0]):
        hits = lax.dot_general(
            pb[ITERS],
            proj[b * LANES : (b + 1) * LANES, :],
            (((1,), (1,)), ((), ())),
            preferred_element_type=F32,
        )
        want = jnp.where(cvib_ref[b : b + 1, :] == v_me, crad_ref[b : b + 1, :], -1)
        chosen = jnp.where(radial == want, hits, 0.0)
        asend[b] = jnp.broadcast_to(jnp.sum(chosen, axis=0, keepdims=True), (8, LANES))

    def send_amp(s, carry):
        i = order(s)
        push(asend.at[i // 2], arecv.at[v_me], amp_s.at[i], amp_r.at[v_me], (k_me, i))
        return carry

    lax.fori_loop(0, NCH, send_amp, 0)

    def take_amp(v, carry):
        pltpu.make_async_copy(tile, arecv.at[v], amp_r.at[v]).wait()
        return carry + arecv[v]

    total = lax.fori_loop(0, NCH, take_amp, jnp.zeros((8, LANES), F32))
    half = amp_ref.shape[1]
    amp_ref[...] = jnp.where(rad % 2 == 1, total[0:1, half:], total[0:1, :half])

    def settle(s, carry):
        pltpu.make_async_copy(fin_ref.at[s], fin_ref.at[s], fin_r.at[s]).wait()
        v, device = holder(s)
        pushed(stage.at[v], pb.at[0, chunk(rad), :], psi_s.at[s], psi_r.at[rad], device)
        pushed(tile, tiles.at[rad], til_s.at[s], til_r.at[rad], device)
        i = order(s)
        pushed(
            fw.at[ITERS + 1, chunk(i), :], fin_ref.at[v_me], fin_s.at[i], fin_r.at[v_me], (k_me, i)
        )
        pushed(asend.at[i // 2], arecv.at[v_me], amp_s.at[i], amp_r.at[v_me], (k_me, i))
        return carry

    lax.fori_loop(0, NCH, settle, 0)

    def settle_halo(n, carry):
        def one(i, carry):
            part_n = pb.at[n, chunk(i), :]
            remote(part_n, lo.at[n, chunk(i), :], lo_s.at[n, i], lo_r.at[n, i], above).wait_send()
            remote(part_n, up.at[n, chunk(i), :], up_s.at[n, i], up_r.at[n, i], below).wait_send()
            return carry

        return lax.fori_loop(0, NCH, one, carry)

    lax.fori_loop(0, ITERS, settle_halo, 0)

    def settle_pot(s, carry):
        i, device = pot_holder(s)
        pushed(pstage.at[i], pot.at[chunk(rad), :], pot_s.at[s], pot_r.at[rad // 2], device)
        c = 2 * s + core
        remote(
            pot.at[chunk(c), :], pot.at[chunk(c), :], sib_s.at[s], sib_r.at[s], sibling
        ).wait_send()
        return carry

    lax.fori_loop(0, NCH // 2, settle_pot, 0)


def per_device(
    psi_start,
    potential,
    basis,
    kinetic,
    radial_factor,
    damping,
    coupling,
    helicity,
    chan_rad,
    chan_vib,
    projector,
):
    _, rdev, nvib, nang = psi_start.shape
    nquad = basis.shape[1]
    nchan = projector.shape[0]
    rows = NCH * rdev
    out_chan = nchan // NCH
    anyspace = pl.BlockSpec(memory_space=pl.ANY)
    smem = pl.BlockSpec(memory_space=pltpu.SMEM)
    vmem = pl.BlockSpec(memory_space=pltpu.VMEM)
    dma = pltpu.SemaphoreType.DMA
    fin, amp = pl.pallas_call(
        kernel,
        name="propagate",
        out_shape=(
            jax.ShapeDtypeStruct((nvib, rdev, nang), F32),
            jax.ShapeDtypeStruct((1, out_chan), F32),
        ),
        in_specs=[anyspace] * 5 + [smem] * 3 + [vmem] * 3,
        out_specs=(anyspace, vmem),
        scratch_shapes=[
            pltpu.VMEM((nang // LANES, rdev * nvib, LANES), F32),
            pltpu.VMEM((nquad // LANES, rdev * nvib, LANES), F32),
            pltpu.VMEM((nang, nquad), BF16),
            pltpu.VMEM((rows, rows), BF16),
            pltpu.VMEM((nchan, nang), BF16),
            pltpu.VMEM((nvib, rdev, nang), BF16),
            pltpu.VMEM((nvib // 2, rdev, nquad), BF16),
            pltpu.VMEM((8, LANES), F32),
            pltpu.VMEM((NCH, 8, LANES), F32),
            pltpu.VMEM((8, LANES), F32),
            pltpu.VMEM((8, LANES), F32),
            pltpu.VMEM((ITERS + 1, rows, nang), BF16),
            pltpu.VMEM((ITERS, rows, nang), BF16),
            pltpu.VMEM((ITERS, rows, nang), BF16),
            pltpu.VMEM((ITERS + 2, rows, nang), F32),
            pltpu.VMEM((rows, nquad), BF16),
            pltpu.VMEM((rows, nquad), BF16),
            pltpu.VMEM((rows, nang), F32),
            pltpu.VMEM((rows, LANES), F32),
            pltpu.VMEM((rows, LANES), F32),
            pltpu.VMEM((nchan // LANES, 8, LANES), F32),
            pltpu.VMEM((NCH, 8, LANES), F32),
            dma((3,)),
            dma((nang // LANES,)),
            dma((nquad // LANES,)),
            dma((NCH,)),
            dma((NCH,)),
            dma((NCH,)),
            dma((NCH,)),
            dma((NCH // 2,)),
            dma((NCH // 2,)),
            dma((NCH // 2,)),
            dma((NCH // 2,)),
            dma((ITERS, NCH)),
            dma((ITERS, NCH)),
            dma((ITERS, NCH)),
            dma((ITERS, NCH)),
            dma,
            dma,
            dma((NCH,)),
            dma((NCH,)),
            dma((NCH,)),
            dma((NCH,)),
        ],
        compiler_params=pltpu.CompilerParams(
            collective_id=0, has_side_effects=True, vmem_limit_bytes=56 * 2**20
        ),
    )(
        psi_start.reshape(rdev * nvib, nang),
        potential.reshape(rdev * nvib, nquad),
        basis,
        kinetic,
        projector,
        radial_factor,
        damping,
        helicity,
        coupling,
        chan_rad.reshape(-1, LANES),
        chan_vib.reshape(-1, LANES),
    )
    return (jnp.transpose(fin, (1, 0, 2))[None], amp)


def solution(mesh):
    placed = (
        P("hel", "rad", None, None),
        P("rad", None, None),
        P(),
        P(),
        P("rad"),
        P("rad"),
        P("hel", None),
        P("hel"),
        P(),
        P(),
        P(),
    )
    return jax.shard_map(
        per_device,
        mesh=mesh,
        in_specs=placed,
        out_specs=(P("hel", "rad", None, None), P("hel", "rad")),
        check_vma=False,
    )
```

```python
import jax
import jax.numpy as jnp
from jax import lax
from jax.experimental import pallas as pl
from jax.experimental.pallas import tpu as pltpu
from jax.sharding import PartitionSpec as P

ITERS = 3
MESH = pl.DeviceIdType.MESH
F32 = jnp.float32
BF16 = jnp.bfloat16
NCH = 16
ZS = 8
LANES = 128


def div(a, b):
    return lax.div(a, jnp.int32(b))


def rem(a, b):
    return lax.rem(a, jnp.int32(b))


def kernel(
    psi_hbm,
    pot_hbm,
    basis_hbm,
    kin_hbm,
    proj_hbm,
    rf_hbm,
    damp_hbm,
    hel_hbm,
    coup_hbm,
    crad_hbm,
    cvib_hbm,
    fin_ref,
    amp_ref,
    rf_ref,
    damp_ref,
    hel_ref,
    coup_ref,
    crad_ref,
    cvib_ref,
    psi_v,
    pot_v,
    basis,
    kin,
    proj,
    stage,
    pstage,
    tile,
    tiles,
    ce,
    cp,
    pb,
    late,
    lo,
    up,
    fw,
    pot,
    scaled,
    tot,
    dmp,
    cen,
    asend,
    arecv,
    kept,
    kept_sem,
    load_sem,
    psi_l,
    pot_l,
    psi_s,
    psi_r,
    til_s,
    til_r,
    pot_s,
    pot_r,
    sib_s,
    sib_r,
    lo_s,
    lo_r,
    up_s,
    up_r,
    cp_s,
    cp_r,
    fin_s,
    fin_r,
    amp_s,
    amp_r,
):
    hel, rad = lax.axis_index("hel"), lax.axis_index("rad")
    x_hi, z = div(hel, ZS), rem(hel, ZS)
    x_lo, y, core = div(rad, 8), rem(div(rad, 2), 4), rem(rad, 2)
    v_me = x_hi * 8 + x_lo * 4 + y
    k_me = core * ZS + z
    column = x_lo * 8 + y * 2
    z_up, z_down = rem(z + 1, ZS), rem(z + ZS - 1, ZS)
    above = (x_hi * ZS + z_up, column + rem(core + div(z + 1, ZS), 2))
    below = (x_hi * ZS + z_down, column + rem(core + 1 - div(z + ZS - 1, ZS), 2))
    sibling = (hel, column + 1 - core)
    rows, nang = pb.shape[1:]
    nquad = pot.shape[1]
    part = rows // NCH

    barrier = pltpu.get_barrier_semaphore()
    for neighbour in (above, below):
        pl.semaphore_signal(barrier, inc=1, device_id=neighbour, device_id_type=MESH)
    def greet(i, carry):
        pl.semaphore_signal(
            barrier, inc=1, device_id=((1 - x_hi) * ZS + z, i), device_id_type=MESH
        )

        @pl.when(i != rad)
        def _():
            pl.semaphore_signal(barrier, inc=1, device_id=(hel, i), device_id_type=MESH)

        return carry

    lax.fori_loop(0, NCH, greet, 0)

    def load_lanes(b, carry):
        cols = pl.ds(pl.multiple_of(b * LANES, LANES), LANES)
        pltpu.make_async_copy(psi_hbm.at[:, cols], psi_v.at[b], psi_l.at[b]).start()
        return carry

    def load_pot_lanes(b, carry):
        cols = pl.ds(pl.multiple_of(b * LANES, LANES), LANES)
        pltpu.make_async_copy(pot_hbm.at[:, cols], pot_v.at[b], pot_l.at[b]).start()
        return carry

    loads = [
        pltpu.make_async_copy(src, dst, load_sem.at[i])
        for i, (src, dst) in enumerate(
            [
                (rf_hbm, rf_ref),
                (damp_hbm, damp_ref),
                (hel_hbm, hel_ref),
                (coup_hbm, coup_ref),
                (kin_hbm, kin),
                (basis_hbm, basis),
                (proj_hbm, proj),
                (crad_hbm, crad_ref),
                (cvib_hbm, cvib_ref),
            ]
        )
    ]
    small_loads, big_loads = loads[:4], loads[4:]
    lax.fori_loop(0, nang // LANES, load_lanes, 0)
    for load in small_loads:
        load.start()
    lax.fori_loop(0, nquad // LANES, load_pot_lanes, 0)
    for load in big_loads:
        load.start()

    def chunk(i):
        return pl.ds(pl.multiple_of(i * part, part), part)

    def remote(src, dst, send, recv, device):
        return pltpu.make_async_remote_copy(
            src_ref=src,
            dst_ref=dst,
            send_sem=send,
            recv_sem=recv,
            device_id=device,
            device_id_type=MESH,
        )

    def is_here(device):
        return (device[0] == hel) & (device[1] == rad)

    def push(src, dst, send, recv, device):
        mine = is_here(device)

        @pl.when(mine)
        def _():
            pltpu.make_async_copy(src, dst, recv).start()

        @pl.when(jnp.logical_not(mine))
        def _():
            remote(src, dst, send, recv, device).start()

    def pushed(src, dst, send, recv, device):
        @pl.when(jnp.logical_not(is_here(device)))
        def _():
            remote(src, dst, send, recv, device).wait_send()

    for load in small_loads:
        load.wait()
    kvalue = hel_ref[...].astype(F32)
    tile[0:1, 0:part] = damp_ref[...]
    tile[1:2, 0:part] = -2.0 * (kvalue * kvalue) * rf_ref[...]
    wide = coup_ref[...].astype(F32)
    for b in range(nang // LANES):
        tile[2 + b : 3 + b, :] = wide[:, b * LANES : (b + 1) * LANES]

    for b in range(nang // LANES):
        cols = slice(b * LANES, (b + 1) * LANES)
        pltpu.make_async_copy(psi_hbm.at[:, cols], psi_v.at[b], psi_l.at[b]).wait()
        for v in range(NCH):
            stage[v, :, cols] = psi_v[b, pl.ds(v, part, stride=NCH), :].astype(BF16)
    pl.semaphore_wait(barrier, 2 * NCH + 1)

    def holder(s):
        v = rem(rad + s, NCH)
        return v, (div(v, 8) * ZS + z, rem(v, 8) * 2 + x_hi)

    def send_psi(s, carry):
        v, device = holder(s)
        push(stage.at[v], pb.at[0, chunk(rad), :], psi_s.at[s], psi_r.at[rad], device)
        return carry

    def send_tile(s, carry):
        v, device = holder(s)
        push(tile, tiles.at[rad], til_s.at[s], til_r.at[rad], device)
        return carry

    lax.fori_loop(0, NCH, send_tile, 0)
    lax.fori_loop(0, NCH, send_psi, 0)

    for b in range(nquad // LANES):
        cols = slice(b * LANES, (b + 1) * LANES)
        pltpu.make_async_copy(pot_hbm.at[:, cols], pot_v.at[b], pot_l.at[b]).wait()
        for i in range(NCH // 2):
            pstage[i, :, cols] = pot_v[b, pl.ds(x_hi * 8 + i, part, stride=NCH), :].astype(BF16)

    half_me = div(rad, 2)

    def pot_holder(s):
        i = rem(half_me + s, 8)
        return i, (hel, 2 * i + core)

    def send_pot(s, carry):
        i, device = pot_holder(s)
        push(pstage.at[i], pot.at[chunk(rad), :], pot_s.at[s], pot_r.at[half_me], device)
        return carry


    lax.fori_loop(0, NCH // 2, send_pot, 0)

    def send_on(n, i):
        remote(
            pb.at[n, chunk(i), :], lo.at[n, chunk(i), :], lo_s.at[n, i], lo_r.at[n, i], above
        ).start()
        remote(
            pb.at[n, chunk(i), :], up.at[n, chunk(i), :], up_s.at[n, i], up_r.at[n, i], below
        ).start()

    def order(s):
        return rem(v_me + NCH - s, NCH)

    def take_psi(s, carry):
        i = order(s)
        pltpu.make_async_copy(stage.at[0], pb.at[0, chunk(i), :], psi_r.at[i]).wait()
        send_on(0, i)
        return carry

    first = order(0)
    pltpu.make_async_copy(tile, tiles.at[first], til_r.at[first]).wait()
    ce[...] = jnp.where(k_me < 2 * ZS - 1, tiles[first], 0.0)
    remote(ce, cp, cp_s, cp_r, above).start()
    lax.fori_loop(0, NCH, take_psi, 0)

    diag = lax.broadcasted_iota(jnp.int32, (part, LANES), 0)
    diag_lane = lax.broadcasted_iota(jnp.int32, (part, LANES), 1)

    def take_pot(s, carry):
        j = rem(half_me + 8 - s, 8)
        i = 2 * j + core
        pltpu.make_async_copy(pstage.at[0], pot.at[chunk(i), :], pot_r.at[j]).wait()
        remote(
            pot.at[chunk(i), :], pot.at[chunk(i), :], sib_s.at[j], sib_r.at[j], sibling
        ).start()
        return carry

    lax.fori_loop(0, NCH // 2, take_pot, 0)

    def take_tile(s, carry):
        i = order(s)
        pltpu.make_async_copy(tile, tiles.at[i], til_r.at[i]).wait()
        return carry

    lax.fori_loop(1, NCH, take_tile, 0)
    for i in range(NCH):
        span = slice(i * part, (i + 1) * part)
        here = diag_lane == diag
        d_row = jnp.broadcast_to(tiles[i, 0:1, :], (part, LANES))
        c_row = jnp.broadcast_to(tiles[i, 1:2, :], (part, LANES))
        d = jnp.sum(jnp.where(here, d_row, 0.0), axis=1, keepdims=True)
        c = jnp.sum(jnp.where(here, c_row, 0.0), axis=1, keepdims=True)
        dmp[span, :] = jnp.broadcast_to(d, (part, LANES))
        cen[span, :] = jnp.broadcast_to(c, (part, LANES))
    asend[...] = jnp.zeros(asend.shape, F32)
    fw[0] = jnp.zeros((rows, nang), F32)
    fw[1] = pb[0].astype(F32)
    for load in big_loads:
        load.wait()

    def take_sib(j, carry):
        i = 2 * j + 1 - core
        pltpu.make_async_copy(pstage.at[0], pot.at[chunk(i), :], sib_r.at[j]).wait()
        return carry

    lax.fori_loop(0, NCH // 2, take_sib, 0)

    def settle_halo(n, i, carry):
        part_n = pb.at[n, chunk(i), :]
        remote(part_n, lo.at[n, chunk(i), :], lo_s.at[n, i], lo_r.at[n, i], above).wait_send()
        remote(part_n, up.at[n, chunk(i), :], up_s.at[n, i], up_r.at[n, i], below).wait_send()
        return carry

    def settle_in(s, carry):
        v, device = holder(s)
        pushed(stage.at[v], pb.at[0, chunk(rad), :], psi_s.at[s], psi_r.at[rad], device)
        pushed(tile, tiles.at[rad], til_s.at[s], til_r.at[rad], device)
        return carry

    def settle_pot(s, carry):
        i, device = pot_holder(s)
        pushed(pstage.at[i], pot.at[chunk(rad), :], pot_s.at[s], pot_r.at[half_me], device)
        c = 2 * s + core
        remote(
            pot.at[chunk(c), :], pot.at[chunk(c), :], sib_s.at[s], sib_r.at[s], sibling
        ).wait_send()
        return carry

    wide_q = 256

    group = 4
    grows = group * part
    in_group = lax.broadcasted_iota(jnp.int32, (grows, LANES), 0)

    def project(g):
        radial = rem(v_me + NCH - g * group - div(in_group, part), NCH) * part + rem(in_group, part)
        block = late[pl.ds(pl.multiple_of(g * grows, grows), grows), :]
        for b in range(0, crad_ref.shape[0], 2):
            hits = lax.dot_general(
                block,
                proj[b * LANES : (b + 2) * LANES, :],
                (((1,), (1,)), ((), ())),
                preferred_element_type=F32,
            )
            for h in range(2):
                line = slice(b + h, b + h + 1)
                want = jnp.where(cvib_ref[line, :] == v_me, crad_ref[line, :], -1)
                chosen = jnp.where(radial == want, hits[:, h * LANES : (h + 1) * LANES], 0.0)
                asend[b + h] += jnp.broadcast_to(
                    jnp.sum(chosen, axis=0, keepdims=True), (8, LANES)
                )

    def step(n, carry):
        for q in range(nquad // wide_q):
            cols = slice(q * wide_q, (q + 1) * wide_q)
            grid = jnp.dot(pb[n], basis[:, cols], preferred_element_type=F32)
            scaled[:, cols] = (grid * pot[:, cols].astype(F32)).astype(BF16)
        for q in range(nang // wide_q):
            cols = slice(q * wide_q, (q + 1) * wide_q)
            tot[:, cols] = jnp.dot(
                kin[...], pb[n, :, cols], preferred_element_type=F32
            ) + lax.dot_general(
                scaled[...],
                basis[cols, :],
                (((1,), (1,)), ((), ())),
                preferred_element_type=F32,
            )

        @pl.when(n == 1)
        def _():
            lax.fori_loop(0, NCH, settle_in, 0)
            lax.fori_loop(0, NCH // 2, settle_pot, 0)

        @pl.when(n >= 1)
        def _():
            lax.fori_loop(0, NCH, lambda i, c: settle_halo(n - 1, i, c), 0)

        @pl.when(n == 0)
        def _():
            remote(ce, cp, cp_s, cp_r, above).wait()

        spare = pltpu.make_async_copy(fw.at[n + 1, 0:8, 0:LANES], kept, kept_sem)
        spare.start()
        spare.wait()
        gain = jnp.where(n == 0, 1.0, 2.0).astype(F32)

        def finish(s, carry):
            i = order(s)
            pltpu.make_async_copy(stage.at[0], lo.at[n, chunk(i), :], lo_r.at[n, i]).wait()
            pltpu.make_async_copy(stage.at[0], up.at[n, chunk(i), :], up_r.at[n, i]).wait()
            d = dmp[chunk(i), :]
            c = cen[chunk(i), :]
            for b in range(nang // LANES):
                cols = slice(b * LANES, (b + 1) * LANES)
                h = (
                    tot[chunk(i), cols]
                    + c * fw[n + 1, chunk(i), cols]
                    + ce[2 + b : 3 + b, :] * up[n, chunk(i), cols].astype(F32)
                    + cp[2 + b : 3 + b, :] * lo[n, chunk(i), cols].astype(F32)
                )
                new = d * (gain * h - d * fw[n, chunk(i), cols])
                fw[n + 2, chunk(i), cols] = new
                pb[n + 1, chunk(i), cols] = new.astype(BF16)

            late[chunk(s), :] = pb[n + 1, chunk(i), :]

            @pl.when(n < ITERS - 1)
            def _():
                send_on(n + 1, i)

            @pl.when(n == ITERS - 1)
            def _():
                push(
                    pb.at[ITERS, chunk(i), :],
                    fin_ref.at[v_me],
                    fin_s.at[i],
                    fin_r.at[v_me],
                    (k_me, i),
                )

                @pl.when(rem(s, group) == group - 1)
                def _():
                    project(div(s, group))

            return carry

        lax.fori_loop(0, NCH, finish, 0)
        return carry

    lax.fori_loop(0, ITERS, step, 0)

    def send_amp(s, carry):
        i = order(s)
        push(asend.at[div(i, 2)], arecv.at[v_me], amp_s.at[i], amp_r.at[v_me], (k_me, i))
        return carry

    lax.fori_loop(0, NCH, send_amp, 0)

    def settle(s, carry):
        i = order(s)
        settle_halo(ITERS - 1, s, carry)
        pushed(
            pb.at[ITERS, chunk(i), :], fin_ref.at[v_me], fin_s.at[i], fin_r.at[v_me], (k_me, i)
        )
        pushed(asend.at[div(i, 2)], arecv.at[v_me], amp_s.at[i], amp_r.at[v_me], (k_me, i))
        return carry

    lax.fori_loop(0, NCH, settle, 0)

    def take_fin(v, carry):
        pltpu.make_async_copy(stage.at[0], fin_ref.at[v], fin_r.at[v]).wait()
        return carry

    lax.fori_loop(0, NCH, take_fin, 0)
    for v in range(NCH):
        pltpu.make_async_copy(tile, arecv.at[v], amp_r.at[v]).wait()
    amp_ref[...] = jnp.sum(arecv[...], axis=0)


def place(fin_hbm, amp_ref, out_hbm, half_ref, fin, out, sem, out_sem):
    load = pltpu.make_async_copy(fin_hbm, fin, sem)
    load.start()
    rad = lax.axis_index("rad")
    half = half_ref.shape[1]
    half_ref[...] = jnp.where(rad % 2 == 1, amp_ref[0:1, half:], amp_ref[0:1, :half])
    nvib, part, nang = fin.shape
    load.wait()
    copies = []
    for b in range(nang // LANES):
        cols = slice(b * LANES, (b + 1) * LANES)
        for v in range(nvib):
            out[b, pl.ds(v, part, stride=nvib), :] = fin[v, :, cols].astype(F32)
        copies.append(pltpu.make_async_copy(out.at[b], out_hbm.at[:, cols], out_sem.at[b]))
        copies[-1].start()
    for copy in copies:
        copy.wait()


def per_device(
    psi_start,
    potential,
    basis,
    kinetic,
    radial_factor,
    damping,
    coupling,
    helicity,
    chan_rad,
    chan_vib,
    projector,
):
    _, rdev, nvib, nang = psi_start.shape
    nquad = basis.shape[1]
    nchan = projector.shape[0]
    rows = NCH * rdev
    out_chan = nchan // NCH
    anyspace = pl.BlockSpec(memory_space=pl.ANY)
    vmem = pl.BlockSpec(memory_space=pltpu.VMEM)
    dma = pltpu.SemaphoreType.DMA
    fin, amp = pl.pallas_call(
        kernel,
        name="propagate",
        out_shape=(
            jax.ShapeDtypeStruct((nvib, rdev, nang), BF16),
            jax.ShapeDtypeStruct((8, LANES), F32),
        ),
        in_specs=[anyspace] * 11,
        out_specs=(anyspace, vmem),
        scratch_shapes=[
            pltpu.VMEM((1, rdev), F32),
            pltpu.VMEM((1, rdev), F32),
            pltpu.VMEM((1, 1), jnp.int32),
            pltpu.VMEM((1, nang), BF16),
            pltpu.VMEM((nchan // LANES, LANES), jnp.int32),
            pltpu.VMEM((nchan // LANES, LANES), jnp.int32),
            pltpu.VMEM((nang // LANES, rdev * nvib, LANES), F32),
            pltpu.VMEM((nquad // LANES, rdev * nvib, LANES), F32),
            pltpu.VMEM((nang, nquad), BF16),
            pltpu.VMEM((rows, rows), BF16),
            pltpu.VMEM((nchan, nang), BF16),
            pltpu.VMEM((nvib, rdev, nang), BF16),
            pltpu.VMEM((nvib // 2, rdev, nquad), BF16),
            pltpu.VMEM((8, LANES), F32),
            pltpu.VMEM((NCH, 8, LANES), F32),
            pltpu.VMEM((8, LANES), F32),
            pltpu.VMEM((8, LANES), F32),
            pltpu.VMEM((ITERS + 1, rows, nang), BF16),
            pltpu.VMEM((rows, nang), BF16),
            pltpu.VMEM((ITERS, rows, nang), BF16),
            pltpu.VMEM((ITERS, rows, nang), BF16),
            pltpu.VMEM((ITERS + 2, rows, nang), F32),
            pltpu.VMEM((rows, nquad), BF16),
            pltpu.VMEM((rows, nquad), BF16),
            pltpu.VMEM((rows, nang), F32),
            pltpu.VMEM((rows, LANES), F32),
            pltpu.VMEM((rows, LANES), F32),
            pltpu.VMEM((nchan // LANES, 8, LANES), F32),
            pltpu.VMEM((NCH, 8, LANES), F32),
            pltpu.VMEM((8, LANES), F32),
            dma,
            dma((9,)),
            dma((nang // LANES,)),
            dma((nquad // LANES,)),
            dma((NCH,)),
            dma((NCH,)),
            dma((NCH,)),
            dma((NCH,)),
            dma((NCH // 2,)),
            dma((NCH // 2,)),
            dma((NCH // 2,)),
            dma((NCH // 2,)),
            dma((ITERS, NCH)),
            dma((ITERS, NCH)),
            dma((ITERS, NCH)),
            dma((ITERS, NCH)),
            dma,
            dma,
            dma((NCH,)),
            dma((NCH,)),
            dma((NCH,)),
            dma((NCH,)),
        ],
        compiler_params=pltpu.CompilerParams(
            collective_id=0, has_side_effects=True, vmem_limit_bytes=56 * 2**20
        ),
    )(
        psi_start.reshape(rdev * nvib, nang),
        potential.reshape(rdev * nvib, nquad),
        basis,
        kinetic,
        projector,
        radial_factor.reshape(1, -1),
        damping.reshape(1, -1),
        helicity.reshape(1, 1),
        coupling,
        chan_rad.reshape(-1, LANES),
        chan_vib.reshape(-1, LANES),
    )
    psi_final, amplitude = pl.pallas_call(
        place,
        name="place",
        out_shape=(
            jax.ShapeDtypeStruct((rows, nang), F32),
            jax.ShapeDtypeStruct((1, out_chan), F32),
        ),
        in_specs=[anyspace, vmem],
        out_specs=(anyspace, vmem),
        scratch_shapes=[
            pltpu.VMEM((nvib, rdev, nang), BF16),
            pltpu.VMEM((nang // LANES, rows, LANES), F32),
            dma,
            dma((nang // LANES,)),
        ],
    )(fin, amp)
    return (psi_final.reshape(1, rdev, nvib, nang), amplitude)


def solution(mesh):
    placed = (
        P("hel", "rad", None, None),
        P("rad", None, None),
        P(),
        P(),
        P("rad"),
        P("rad"),
        P("hel", None),
        P("hel"),
        P(),
        P(),
        P(),
    )
    return jax.shard_map(
        per_device,
        mesh=mesh,
        in_specs=placed,
        out_specs=(P("hel", "rad", None, None), P("hel", "rad")),
        check_vma=False,
    )
```

```python
import jax
import jax.numpy as jnp
from jax import lax
from jax.experimental import pallas as pl
from jax.experimental.pallas import tpu as pltpu
from jax.sharding import PartitionSpec as P

ITERS = 3
MESH = pl.DeviceIdType.MESH
F32 = jnp.float32
BF16 = jnp.bfloat16
NCH = 16
ZS = 8
LANES = 128


def div(a, b):
    return lax.div(a, jnp.int32(b))


def rem(a, b):
    return lax.rem(a, jnp.int32(b))


def kernel(
    psi_hbm,
    pot_hbm,
    basis_hbm,
    kin_hbm,
    proj_hbm,
    rf_hbm,
    damp_hbm,
    hel_hbm,
    coup_hbm,
    crad_hbm,
    cvib_hbm,
    fin_ref,
    amp_ref,
    rf_ref,
    damp_ref,
    hel_ref,
    coup_ref,
    crad_ref,
    cvib_ref,
    psi_v,
    pot_v,
    basis,
    kin,
    proj,
    stage,
    pstage,
    tile,
    tiles,
    ce,
    cp,
    pb,
    late,
    lo,
    up,
    fw,
    pot,
    scaled,
    tot,
    dmp,
    cen,
    asend,
    arecv,
    load_sem,
    psi_l,
    pot_l,
    psi_s,
    psi_r,
    til_s,
    til_r,
    pot_s,
    pot_r,
    sib_s,
    sib_r,
    lo_s,
    lo_r,
    up_s,
    up_r,
    cp_s,
    cp_r,
    fin_s,
    fin_r,
    amp_s,
    amp_r,
):
    hel, rad = lax.axis_index("hel"), lax.axis_index("rad")
    x_hi, z = div(hel, ZS), rem(hel, ZS)
    x_lo, y, core = div(rad, 8), rem(div(rad, 2), 4), rem(rad, 2)
    v_me = x_hi * 8 + x_lo * 4 + y
    k_me = core * ZS + z
    column = x_lo * 8 + y * 2
    z_up, z_down = rem(z + 1, ZS), rem(z + ZS - 1, ZS)
    above = (x_hi * ZS + z_up, column + rem(core + div(z + 1, ZS), 2))
    below = (x_hi * ZS + z_down, column + rem(core + 1 - div(z + ZS - 1, ZS), 2))
    sibling = (hel, column + 1 - core)
    rows, nang = pb.shape[1:]
    nquad = pot.shape[1]
    part = rows // NCH

    barrier = pltpu.get_barrier_semaphore()
    for neighbour in (above, below):
        pl.semaphore_signal(barrier, inc=1, device_id=neighbour, device_id_type=MESH)
    def greet(i, carry):
        pl.semaphore_signal(
            barrier, inc=1, device_id=((1 - x_hi) * ZS + z, i), device_id_type=MESH
        )

        @pl.when(i != rad)
        def _():
            pl.semaphore_signal(barrier, inc=1, device_id=(hel, i), device_id_type=MESH)

        return carry

    lax.fori_loop(0, NCH, greet, 0)

    def load_lanes(b, carry):
        cols = pl.ds(pl.multiple_of(b * LANES, LANES), LANES)
        pltpu.make_async_copy(psi_hbm.at[:, cols], psi_v.at[b], psi_l.at[b]).start()
        return carry

    def load_pot_lanes(b, carry):
        cols = pl.ds(pl.multiple_of(b * LANES, LANES), LANES)
        pltpu.make_async_copy(pot_hbm.at[:, cols], pot_v.at[b], pot_l.at[b]).start()
        return carry

    loads = [
        pltpu.make_async_copy(src, dst, load_sem.at[i])
        for i, (src, dst) in enumerate(
            [
                (rf_hbm, rf_ref),
                (damp_hbm, damp_ref),
                (hel_hbm, hel_ref),
                (coup_hbm, coup_ref),
                (kin_hbm, kin),
                (basis_hbm, basis),
                (proj_hbm, proj),
                (crad_hbm, crad_ref),
                (cvib_hbm, cvib_ref),
            ]
        )
    ]
    small_loads, big_loads = loads[:4], loads[4:]
    lax.fori_loop(0, nang // LANES, load_lanes, 0)
    for load in small_loads:
        load.start()
    lax.fori_loop(0, nquad // LANES, load_pot_lanes, 0)
    for load in big_loads:
        load.start()

    def chunk(i):
        return pl.ds(pl.multiple_of(i * part, part), part)

    def remote(src, dst, send, recv, device):
        return pltpu.make_async_remote_copy(
            src_ref=src,
            dst_ref=dst,
            send_sem=send,
            recv_sem=recv,
            device_id=device,
            device_id_type=MESH,
        )

    def is_here(device):
        return (device[0] == hel) & (device[1] == rad)

    def push(src, dst, send, recv, device):
        mine = is_here(device)

        @pl.when(mine)
        def _():
            pltpu.make_async_copy(src, dst, recv).start()

        @pl.when(jnp.logical_not(mine))
        def _():
            remote(src, dst, send, recv, device).start()

    def pushed(src, dst, send, recv, device):
        @pl.when(jnp.logical_not(is_here(device)))
        def _():
            remote(src, dst, send, recv, device).wait_send()

    for load in small_loads:
        load.wait()
    kvalue = hel_ref[...].astype(F32)
    tile[0:1, 0:part] = damp_ref[...]
    tile[1:2, 0:part] = -2.0 * (kvalue * kvalue) * rf_ref[...]
    wide = coup_ref[...].astype(F32)
    for b in range(nang // LANES):
        tile[2 + b : 3 + b, :] = wide[:, b * LANES : (b + 1) * LANES]

    for b in range(nang // LANES):
        cols = slice(b * LANES, (b + 1) * LANES)
        pltpu.make_async_copy(psi_hbm.at[:, cols], psi_v.at[b], psi_l.at[b]).wait()
        for v in range(NCH):
            stage[v, :, cols] = psi_v[b, pl.ds(v, part, stride=NCH), :].astype(BF16)
    pl.semaphore_wait(barrier, 2 * NCH + 1)

    def holder(s):
        v = rem(rad + s, NCH)
        return v, (div(v, 8) * ZS + z, rem(v, 8) * 2 + x_hi)

    def send_psi(s, carry):
        v, device = holder(s)
        push(stage.at[v], pb.at[0, chunk(rad), :], psi_s.at[s], psi_r.at[rad], device)
        return carry

    def send_tile(s, carry):
        v, device = holder(s)
        push(tile, tiles.at[rad], til_s.at[s], til_r.at[rad], device)
        return carry

    lax.fori_loop(0, NCH, send_tile, 0)
    lax.fori_loop(0, NCH, send_psi, 0)

    for b in range(nquad // LANES):
        cols = slice(b * LANES, (b + 1) * LANES)
        pltpu.make_async_copy(pot_hbm.at[:, cols], pot_v.at[b], pot_l.at[b]).wait()
        for i in range(NCH // 2):
            pstage[i, :, cols] = pot_v[b, pl.ds(x_hi * 8 + i, part, stride=NCH), :].astype(BF16)

    half_me = div(rad, 2)

    def pot_holder(s):
        i = rem(half_me + s, 8)
        return i, (hel, 2 * i + core)

    def send_pot(s, carry):
        i, device = pot_holder(s)
        push(pstage.at[i], pot.at[chunk(rad), :], pot_s.at[s], pot_r.at[half_me], device)
        return carry


    lax.fori_loop(0, NCH // 2, send_pot, 0)

    def send_on(n, i):
        remote(
            pb.at[n, chunk(i), :], lo.at[n, chunk(i), :], lo_s.at[n, i], lo_r.at[n, i], above
        ).start()
        remote(
            pb.at[n, chunk(i), :], up.at[n, chunk(i), :], up_s.at[n, i], up_r.at[n, i], below
        ).start()

    def order(s):
        return rem(v_me + NCH - s, NCH)

    def take_psi(s, carry):
        i = order(s)
        pltpu.make_async_copy(stage.at[0], pb.at[0, chunk(i), :], psi_r.at[i]).wait()
        send_on(0, i)
        return carry

    first = order(0)
    pltpu.make_async_copy(tile, tiles.at[first], til_r.at[first]).wait()
    ce[...] = jnp.where(k_me < 2 * ZS - 1, tiles[first], 0.0)
    remote(ce, cp, cp_s, cp_r, above).start()
    lax.fori_loop(0, NCH, take_psi, 0)

    diag = lax.broadcasted_iota(jnp.int32, (part, LANES), 0)
    diag_lane = lax.broadcasted_iota(jnp.int32, (part, LANES), 1)

    def take_pot(s, carry):
        j = rem(half_me + 8 - s, 8)
        i = 2 * j + core
        pltpu.make_async_copy(pstage.at[0], pot.at[chunk(i), :], pot_r.at[j]).wait()
        remote(
            pot.at[chunk(i), :], pot.at[chunk(i), :], sib_s.at[j], sib_r.at[j], sibling
        ).start()
        return carry

    lax.fori_loop(0, NCH // 2, take_pot, 0)

    def take_tile(s, carry):
        i = order(s)
        pltpu.make_async_copy(tile, tiles.at[i], til_r.at[i]).wait()
        return carry

    lax.fori_loop(1, NCH, take_tile, 0)
    for i in range(NCH):
        span = slice(i * part, (i + 1) * part)
        here = diag_lane == diag
        d_row = jnp.broadcast_to(tiles[i, 0:1, :], (part, LANES))
        c_row = jnp.broadcast_to(tiles[i, 1:2, :], (part, LANES))
        d = jnp.sum(jnp.where(here, d_row, 0.0), axis=1, keepdims=True)
        c = jnp.sum(jnp.where(here, c_row, 0.0), axis=1, keepdims=True)
        dmp[span, :] = jnp.broadcast_to(d, (part, LANES))
        cen[span, :] = jnp.broadcast_to(c, (part, LANES))
    asend[...] = jnp.zeros(asend.shape, F32)
    fw[0] = jnp.zeros((rows, nang), F32)
    fw[1] = pb[0].astype(F32)
    for load in big_loads:
        load.wait()

    def take_sib(j, carry):
        i = 2 * j + 1 - core
        pltpu.make_async_copy(pstage.at[0], pot.at[chunk(i), :], sib_r.at[j]).wait()
        return carry

    lax.fori_loop(0, NCH // 2, take_sib, 0)

    def settle_halo(n, i, carry):
        part_n = pb.at[n, chunk(i), :]
        remote(part_n, lo.at[n, chunk(i), :], lo_s.at[n, i], lo_r.at[n, i], above).wait_send()
        remote(part_n, up.at[n, chunk(i), :], up_s.at[n, i], up_r.at[n, i], below).wait_send()
        return carry

    def settle_in(s, carry):
        v, device = holder(s)
        pushed(stage.at[v], pb.at[0, chunk(rad), :], psi_s.at[s], psi_r.at[rad], device)
        pushed(tile, tiles.at[rad], til_s.at[s], til_r.at[rad], device)
        return carry

    def settle_pot(s, carry):
        i, device = pot_holder(s)
        pushed(pstage.at[i], pot.at[chunk(rad), :], pot_s.at[s], pot_r.at[half_me], device)
        c = 2 * s + core
        remote(
            pot.at[chunk(c), :], pot.at[chunk(c), :], sib_s.at[s], sib_r.at[s], sibling
        ).wait_send()
        return carry

    wide_q = 256

    group = 4
    grows = group * part
    in_group = lax.broadcasted_iota(jnp.int32, (grows, LANES), 0)

    def project(g):
        radial = rem(v_me + NCH - g * group - div(in_group, part), NCH) * part + rem(in_group, part)
        block = late[pl.ds(pl.multiple_of(g * grows, grows), grows), :]
        for b in range(0, crad_ref.shape[0], 2):
            hits = lax.dot_general(
                block,
                proj[b * LANES : (b + 2) * LANES, :],
                (((1,), (1,)), ((), ())),
                preferred_element_type=F32,
            )
            for h in range(2):
                line = slice(b + h, b + h + 1)
                want = jnp.where(cvib_ref[line, :] == v_me, crad_ref[line, :], -1)
                chosen = jnp.where(radial == want, hits[:, h * LANES : (h + 1) * LANES], 0.0)
                asend[b + h] += jnp.broadcast_to(
                    jnp.sum(chosen, axis=0, keepdims=True), (8, LANES)
                )

    def step(n, carry):
        for q in range(nquad // wide_q):
            cols = slice(q * wide_q, (q + 1) * wide_q)
            grid = jnp.dot(pb[n], basis[:, cols], preferred_element_type=F32)
            scaled[:, cols] = (grid * pot[:, cols].astype(F32)).astype(BF16)
        for q in range(nang // wide_q):
            cols = slice(q * wide_q, (q + 1) * wide_q)
            tot[:, cols] = jnp.dot(
                kin[...], pb[n, :, cols], preferred_element_type=F32
            ) + lax.dot_general(
                scaled[...],
                basis[cols, :],
                (((1,), (1,)), ((), ())),
                preferred_element_type=F32,
            )

        if n == 1:
            lax.fori_loop(0, NCH, settle_in, 0)
            lax.fori_loop(0, NCH // 2, settle_pot, 0)

        if n >= 1:
            lax.fori_loop(0, NCH, lambda i, c: settle_halo(n - 1, i, c), 0)

        if n == 0:
            remote(ce, cp, cp_s, cp_r, above).wait()

        gain = 1.0 if n == 0 else 2.0

        def finish(s, carry):
            i = order(s)
            pltpu.make_async_copy(stage.at[0], lo.at[n, chunk(i), :], lo_r.at[n, i]).wait()
            pltpu.make_async_copy(stage.at[0], up.at[n, chunk(i), :], up_r.at[n, i]).wait()
            d = dmp[chunk(i), :]
            c = cen[chunk(i), :]
            for b in range(nang // LANES):
                cols = slice(b * LANES, (b + 1) * LANES)
                h = (
                    tot[chunk(i), cols]
                    + c * fw[n + 1, chunk(i), cols]
                    + ce[2 + b : 3 + b, :] * up[n, chunk(i), cols].astype(F32)
                    + cp[2 + b : 3 + b, :] * lo[n, chunk(i), cols].astype(F32)
                )
                new = d * (gain * h - d * fw[n, chunk(i), cols])
                fw[n + 2, chunk(i), cols] = new
                pb[n + 1, chunk(i), cols] = new.astype(BF16)

            if n == ITERS - 1:
                late[chunk(s), :] = pb[n + 1, chunk(i), :]

            if n < ITERS - 1:
                send_on(n + 1, i)
            else:
                push(
                    pb.at[ITERS, chunk(i), :],
                    fin_ref.at[v_me],
                    fin_s.at[i],
                    fin_r.at[v_me],
                    (k_me, i),
                )

                @pl.when(rem(s, group) == group - 1)
                def _():
                    project(div(s, group))

            return carry

        lax.fori_loop(0, NCH, finish, 0)
        return carry

    for n in range(ITERS):
        step(n, 0)

    def send_amp(s, carry):
        i = order(s)
        push(asend.at[div(i, 2)], arecv.at[v_me], amp_s.at[i], amp_r.at[v_me], (k_me, i))
        return carry

    lax.fori_loop(0, NCH, send_amp, 0)

    def settle(s, carry):
        i = order(s)
        settle_halo(ITERS - 1, s, carry)
        pushed(
            pb.at[ITERS, chunk(i), :], fin_ref.at[v_me], fin_s.at[i], fin_r.at[v_me], (k_me, i)
        )
        pushed(asend.at[div(i, 2)], arecv.at[v_me], amp_s.at[i], amp_r.at[v_me], (k_me, i))
        return carry

    lax.fori_loop(0, NCH, settle, 0)

    def take_fin(v, carry):
        pltpu.make_async_copy(stage.at[0], fin_ref.at[v], fin_r.at[v]).wait()
        return carry

    lax.fori_loop(0, NCH, take_fin, 0)
    for v in range(NCH):
        pltpu.make_async_copy(tile, arecv.at[v], amp_r.at[v]).wait()
    amp_ref[...] = jnp.sum(arecv[...], axis=0)


def place(fin_hbm, amp_ref, out_hbm, half_ref, fin, out, sem, out_sem):
    load = pltpu.make_async_copy(fin_hbm, fin, sem)
    load.start()
    rad = lax.axis_index("rad")
    half = half_ref.shape[1]
    half_ref[...] = jnp.where(rad % 2 == 1, amp_ref[0:1, half:], amp_ref[0:1, :half])
    nvib, part, nang = fin.shape
    load.wait()
    copies = []
    for b in range(nang // LANES):
        cols = slice(b * LANES, (b + 1) * LANES)
        for v in range(nvib):
            out[b, pl.ds(v, part, stride=nvib), :] = fin[v, :, cols].astype(F32)
        copies.append(pltpu.make_async_copy(out.at[b], out_hbm.at[:, cols], out_sem.at[b]))
        copies[-1].start()
    for copy in copies:
        copy.wait()


def per_device(
    psi_start,
    potential,
    basis,
    kinetic,
    radial_factor,
    damping,
    coupling,
    helicity,
    chan_rad,
    chan_vib,
    projector,
):
    _, rdev, nvib, nang = psi_start.shape
    nquad = basis.shape[1]
    nchan = projector.shape[0]
    rows = NCH * rdev
    out_chan = nchan // NCH
    anyspace = pl.BlockSpec(memory_space=pl.ANY)
    vmem = pl.BlockSpec(memory_space=pltpu.VMEM)
    dma = pltpu.SemaphoreType.DMA
    fin, amp = pl.pallas_call(
        kernel,
        name="propagate",
        out_shape=(
            jax.ShapeDtypeStruct((nvib, rdev, nang), BF16),
            jax.ShapeDtypeStruct((8, LANES), F32),
        ),
        in_specs=[anyspace] * 11,
        out_specs=(anyspace, vmem),
        scratch_shapes=[
            pltpu.VMEM((1, rdev), F32),
            pltpu.VMEM((1, rdev), F32),
            pltpu.VMEM((1, 1), jnp.int32),
            pltpu.VMEM((1, nang), BF16),
            pltpu.VMEM((nchan // LANES, LANES), jnp.int32),
            pltpu.VMEM((nchan // LANES, LANES), jnp.int32),
            pltpu.VMEM((nang // LANES, rdev * nvib, LANES), F32),
            pltpu.VMEM((nquad // LANES, rdev * nvib, LANES), F32),
            pltpu.VMEM((nang, nquad), BF16),
            pltpu.VMEM((rows, rows), BF16),
            pltpu.VMEM((nchan, nang), BF16),
            pltpu.VMEM((nvib, rdev, nang), BF16),
            pltpu.VMEM((nvib // 2, rdev, nquad), BF16),
            pltpu.VMEM((8, LANES), F32),
            pltpu.VMEM((NCH, 8, LANES), F32),
            pltpu.VMEM((8, LANES), F32),
            pltpu.VMEM((8, LANES), F32),
            pltpu.VMEM((ITERS + 1, rows, nang), BF16),
            pltpu.VMEM((rows, nang), BF16),
            pltpu.VMEM((ITERS, rows, nang), BF16),
            pltpu.VMEM((ITERS, rows, nang), BF16),
            pltpu.VMEM((ITERS + 2, rows, nang), F32),
            pltpu.VMEM((rows, nquad), BF16),
            pltpu.VMEM((rows, nquad), BF16),
            pltpu.VMEM((rows, nang), F32),
            pltpu.VMEM((rows, LANES), F32),
            pltpu.VMEM((rows, LANES), F32),
            pltpu.VMEM((nchan // LANES, 8, LANES), F32),
            pltpu.VMEM((NCH, 8, LANES), F32),
            dma((9,)),
            dma((nang // LANES,)),
            dma((nquad // LANES,)),
            dma((NCH,)),
            dma((NCH,)),
            dma((NCH,)),
            dma((NCH,)),
            dma((NCH // 2,)),
            dma((NCH // 2,)),
            dma((NCH // 2,)),
            dma((NCH // 2,)),
            dma((ITERS, NCH)),
            dma((ITERS, NCH)),
            dma((ITERS, NCH)),
            dma((ITERS, NCH)),
            dma,
            dma,
            dma((NCH,)),
            dma((NCH,)),
            dma((NCH,)),
            dma((NCH,)),
        ],
        compiler_params=pltpu.CompilerParams(
            collective_id=0, has_side_effects=True, vmem_limit_bytes=56 * 2**20
        ),
    )(
        psi_start.reshape(rdev * nvib, nang),
        potential.reshape(rdev * nvib, nquad),
        basis,
        kinetic,
        projector,
        radial_factor.reshape(1, -1),
        damping.reshape(1, -1),
        helicity.reshape(1, 1),
        coupling,
        chan_rad.reshape(-1, LANES),
        chan_vib.reshape(-1, LANES),
    )
    psi_final, amplitude = pl.pallas_call(
        place,
        name="place",
        out_shape=(
            jax.ShapeDtypeStruct((rows, nang), F32),
            jax.ShapeDtypeStruct((1, out_chan), F32),
        ),
        in_specs=[anyspace, vmem],
        out_specs=(anyspace, vmem),
        scratch_shapes=[
            pltpu.VMEM((nvib, rdev, nang), BF16),
            pltpu.VMEM((nang // LANES, rows, LANES), F32),
            dma,
            dma((nang // LANES,)),
        ],
    )(fin, amp)
    return (psi_final.reshape(1, rdev, nvib, nang), amplitude)


def solution(mesh):
    placed = (
        P("hel", "rad", None, None),
        P("rad", None, None),
        P(),
        P(),
        P("rad"),
        P("rad"),
        P("hel", None),
        P("hel"),
        P(),
        P(),
        P(),
    )
    return jax.shard_map(
        per_device,
        mesh=mesh,
        in_specs=placed,
        out_specs=(P("hel", "rad", None, None), P("hel", "rad")),
        check_vma=False,
    )
```
